512 devices in a mesh: date: 32 (over z_hi, y, x), swath: 16 (over z_lo, core).
Axes of the slice: x: 4, y: 4, z: 16 (z_hi: 2, z_lo: 8; z = z_hi * 8 + z_lo), core: 2. Of those that a mesh axis runs over, the one named last changes fastest.
Arguments:
- raw_echo: bfloat16 [32, 2, 1024, 2048], P('date', None, 'swath'), may hold values from -8 to 8
- range_rate: float32 [], replicated, may hold values from 0.5 to 1
- azimuth_rate: float32 [2048], P('swath'), may hold values from 0.25 to 1
- line_offset: int32 [32], P('date'), may hold values from 0 to 24, as said below
- frac_shift: float32 [32], P('date'), may hold values from 0 to 1
Outputs:
- coregistered: bfloat16 [32, 2, 1024, 2048], P('date', None, 'swath')
- coherence: bfloat16 [32, 2, 2, 1024, 2048], P('date', None, None, 'swath')
The draws below stay inside these ranges and needn't reach their ends.
Inputs may be any that keep to these rules, and one draw needn't show every extreme that they name: `line_offset`: one date has offset 24 and another has offset 0.
All inputs are finite; a program needn't handle non-finite values.
Results may differ from the reference program's by a relative error of at most 0.0076.
Values may be sent and summed in bfloat16 or wider, within the bound.
A program may use at most 64 MiB of HBM per device.

```python
import math
import jax
import jax.numpy as jnp
from jax import lax

AZ = 1024
RG = 2048
TAPS = 8
MAX_OFF = 24
WIN_AZ = 11
WIN_RG = 5
SPAN = 2
DATES = 32


def offsets_from(key):
    first_key, second_key = jax.random.split(jax.random.fold_in(key, 5))
    drawn = jax.random.randint(first_key, (DATES,), 0, MAX_OFF + 1, dtype=jnp.int32)
    shuffled = jax.random.permutation(second_key, DATES)
    drawn = drawn.at[shuffled[0]].set(MAX_OFF)
    return drawn.at[shuffled[1]].set(0)


def draw_line_offset(key, part):
    return offsets_from(key)


def draw_raw_echo(key, part):
    offsets = offsets_from(key)
    scene_key, noise_key, turn_key = jax.random.split(jax.random.fold_in(key, 9), 3)
    scene_part = jax.random.normal(scene_key, (2, AZ, RG), jnp.float32)
    noise_part = jax.random.normal(noise_key, (DATES, 2, AZ, RG), jnp.float32)
    coherent_weight = 0.8
    noise_weight = math.sqrt(1.0 - coherent_weight * coherent_weight)
    turn_angles = jax.random.uniform(turn_key, (DATES,), jnp.float32, -math.pi, math.pi)

    def place(line_shift, turn_angle):
        rolled = jnp.roll(scene_part, line_shift, axis=1)
        cosine = jnp.cos(turn_angle)
        sine_val = jnp.sin(turn_angle)
        return jnp.stack([cosine * rolled[0] - sine_val * rolled[1], sine_val * rolled[0] + cosine * rolled[1]])
    aligned = jax.vmap(place)(offsets, turn_angles)
    blended = coherent_weight * aligned + noise_weight * noise_part
    return jnp.clip(blended, -8.0, 8.0).astype(jnp.bfloat16)


def block_levels(own_key, shape, cuts, least, largest):
    loudness, own = 1.0, jax.random.fold_in(own_key, 6)
    for dim, shards_of in cuts:
        draws = jnp.exp(jax.random.uniform(jax.random.fold_in(own, dim), (shards_of,), jnp.float32, least / len(cuts), largest / len(cuts)))
        loudness = loudness * jnp.repeat(draws, shape[dim] // shards_of).reshape([-1 if axis == dim else 1 for axis in range(len(shape))])
    return loudness


def setup_inputs(seed: int = 0) -> dict:
    key_of = jax.random.split(jax.random.key(seed), 6)
    return {
        "raw_echo": draw_raw_echo(jax.random.fold_in(key_of[5], 71), 0),
        "range_rate": jnp.clip(jax.random.uniform(key_of[1], (), jnp.float32, 0.5, 1.0), 0.5, 1.0),
        "azimuth_rate": jnp.clip(jnp.exp(math.log(1.0) - 1.3862944 * jax.random.uniform(key_of[2], (RG,), jnp.float32) ** block_levels(key_of[2], (RG,), ((0, 16),), -0.2, 0.2)), 0.25, 1.0),
        "line_offset": draw_line_offset(jax.random.fold_in(key_of[5], 71), 0),
        "frac_shift": jnp.clip(1.0 * jax.random.uniform(key_of[4], (DATES,), jnp.float32) ** block_levels(key_of[4], (DATES,), ((0, 32),), -0.2, 0.2), 0.0, 1.0),
    }


two_pi = 2.0 * math.pi
epsilon = 1e-06

def exact_dot(left, right):
    return jnp.dot(left.astype(jnp.float32), right.astype(jnp.float32), precision=lax.Precision.HIGHEST, preferred_element_type=jnp.float32)

def chirp_block(range_rate, row_count, col_count):
    pulse_len = RG // 2
    row_ids = lax.broadcasted_iota(jnp.int32, (row_count, col_count), 0)
    col_ids = lax.broadcasted_iota(jnp.int32, (row_count, col_count), 1)
    lag_ids = row_ids - col_ids
    inside = (lag_ids >= 0) & (lag_ids < pulse_len)
    offset = (lag_ids.astype(jnp.float32) - 0.5 * pulse_len) / pulse_len
    phase_arg = math.pi * pulse_len * range_rate * offset * offset
    amplitude = 1.0 / math.sqrt(pulse_len)
    real_tab = jnp.where(inside, jnp.cos(phase_arg) * amplitude, 0.0).astype(jnp.bfloat16)
    imag_tab = jnp.where(inside, -jnp.sin(phase_arg) * amplitude, 0.0).astype(jnp.bfloat16)
    return (real_tab, imag_tab)

def range_compress(echo_lines, range_rate, product):
    pulse_len = RG // 2
    block_size = min(RG, 256)
    real_tab, imag_tab = chirp_block(range_rate, pulse_len + block_size, block_size)
    line_count = echo_lines.shape[1]
    stacked = echo_lines.reshape(2 * line_count, RG)
    extended = jnp.concatenate([stacked, stacked[:, :pulse_len]], axis=1)

    def one_block(block_id):
        window = lax.dynamic_slice_in_dim(extended, block_id * block_size, pulse_len + block_size, 1)
        with_real = product(window, real_tab)
        with_imag = product(window, imag_tab)
        real_out = with_real[:line_count] - with_imag[line_count:]
        imag_out = with_imag[:line_count] + with_real[line_count:]
        return jnp.stack([real_out, imag_out])
    blocks = lax.map(one_block, jnp.arange(RG // block_size, dtype=jnp.int32))
    return blocks.transpose(1, 2, 0, 3).reshape(2, line_count, RG)

def fourier_rows(first_row, row_count, length):
    row_ids = lax.broadcasted_iota(jnp.int32, (row_count, length), 0) + first_row
    col_ids = lax.broadcasted_iota(jnp.int32, (row_count, length), 1)
    turn_angle = (row_ids * col_ids % length).astype(jnp.float32) * (two_pi / length)
    amplitude = 1.0 / math.sqrt(length)
    return ((jnp.cos(turn_angle) * amplitude).astype(jnp.bfloat16), (-jnp.sin(turn_angle) * amplitude).astype(jnp.bfloat16))

def azimuth_compress(columns, azimuth_rate, product):
    col_count = columns.shape[2]
    joined = jnp.concatenate([columns[0], columns[1]], axis=1)
    block_size = min(AZ, 256)
    block_ids = jnp.arange(AZ // block_size, dtype=jnp.int32)

    def forward_block(block_id):
        first_row = block_id * block_size
        real_tab, imag_tab = fourier_rows(first_row, block_size, AZ)
        with_real = product(real_tab, joined)
        with_imag = product(imag_tab, joined)
        spectrum_re = with_real[:, :col_count] - with_imag[:, col_count:]
        spectrum_im = with_real[:, col_count:] + with_imag[:, :col_count]
        freq_ids = lax.broadcasted_iota(jnp.int32, (block_size, 1), 0) + first_row
        centered = ((freq_ids + AZ // 2) % AZ - AZ // 2).astype(jnp.float32) / AZ
        phase_arg = math.pi * AZ * azimuth_rate[None, :] * centered * centered
        filter_re = jnp.cos(phase_arg)
        filter_im = jnp.sin(phase_arg)
        out_re = spectrum_re * filter_re - spectrum_im * filter_im
        out_im = spectrum_re * filter_im + spectrum_im * filter_re
        return jnp.concatenate([out_re, out_im], axis=1).astype(jnp.bfloat16)
    filtered = lax.map(forward_block, block_ids).reshape(AZ, 2 * col_count)

    def inverse_block(block_id):
        real_tab, imag_tab = fourier_rows(block_id * block_size, block_size, AZ)
        with_real = product(real_tab, filtered)
        with_imag = product(imag_tab, filtered)
        focus_re = with_real[:, :col_count] + with_imag[:, col_count:]
        focus_im = with_real[:, col_count:] - with_imag[:, :col_count]
        return jnp.stack([focus_re, focus_im]).astype(jnp.bfloat16)
    pieces = lax.map(inverse_block, block_ids)
    return pieces.transpose(1, 0, 2, 3).reshape(2, AZ, col_count)

def kernel_taps(fraction):
    half_taps = TAPS // 2
    position = jnp.arange(TAPS, dtype=jnp.int32).astype(jnp.float32) - (half_taps - 1) - fraction
    return jnp.sinc(position) * (0.5 + 0.5 * jnp.cos(math.pi * position / half_taps))

def interpolate(window, tap_weights, out_rows):
    running = tap_weights[0] * window[:, 0:out_rows].astype(jnp.float32)
    for tap_id in range(1, TAPS):
        running = running + tap_weights[tap_id] * window[:, tap_id:tap_id + out_rows].astype(jnp.float32)
    return running.astype(jnp.bfloat16)

def own_power(block_data):
    as_float = block_data.astype(jnp.float32)
    return as_float[0] * as_float[0] + as_float[1] * as_float[1]

def pair_terms(own_block, other_block):
    own_f = own_block.astype(jnp.float32)
    other_f = other_block.astype(jnp.float32)
    cross_re = own_f[0] * other_f[0] + own_f[1] * other_f[1]
    cross_im = own_f[1] * other_f[0] - own_f[0] * other_f[1]
    power_b = other_f[0] * other_f[0] + other_f[1] * other_f[1]
    return jnp.stack([cross_re, cross_im, power_b])

def box_sum(values, out_rows):
    half_rg = WIN_RG // 2
    padded = jnp.pad(values, ((0, 0), (0, 0), (half_rg, half_rg)))
    sample_count = values.shape[2]
    across = padded[:, :, 0:sample_count]
    for offset_id in range(1, WIN_RG):
        across = across + padded[:, :, offset_id:offset_id + sample_count]
    running = across[:, 0:out_rows]
    for offset_id in range(1, WIN_AZ):
        running = running + across[:, offset_id:offset_id + out_rows]
    return running

def coherence_of(box_terms, power_box):
    denominator = jnp.sqrt(power_box * box_terms[2] + epsilon)
    return jnp.stack([box_terms[0] / denominator, box_terms[1] / denominator]).astype(jnp.bfloat16)

def reference(raw_echo, range_rate, azimuth_rate, line_offset, frac_shift):
    rim_lines = MAX_OFF + TAPS - 1

    def focus_date(date_id):
        compressed = range_compress(raw_echo[date_id], range_rate, exact_dot).astype(jnp.bfloat16)
        focused = azimuth_compress(compressed, azimuth_rate, exact_dot)
        extended = jnp.concatenate([focused, focused[:, :rim_lines]], axis=1)
        window = lax.dynamic_slice_in_dim(extended, line_offset[date_id].astype(jnp.int32), AZ + TAPS - 1, 1)
        return interpolate(window, kernel_taps(frac_shift[date_id]), AZ)
    date_ids = jnp.arange(DATES, dtype=jnp.int32)
    coregistered = lax.map(focus_date, date_ids)
    half_win = WIN_AZ // 2
    bordered = jnp.pad(coregistered, ((0, 0), (0, 0), (half_win, half_win), (0, 0)))

    def pair_date(date_id):
        own_block = bordered[date_id]
        power_box = box_sum(own_power(own_block)[None], AZ)[0]
        results = []
        for step_id in range(SPAN):
            partner = bordered[(date_id + step_id + 1) % DATES]
            results.append(coherence_of(box_sum(pair_terms(own_block, partner), AZ), power_box))
        return jnp.stack(results)
    coherence = lax.map(pair_date, date_ids)
    return (coregistered, coherence)
```

```python
import functools
import math

import numpy as np
import jax
import jax.numpy as jnp
from jax import lax
from jax.experimental import pallas as pl
from jax.experimental.pallas import tpu as pltpu
from jax.sharding import PartitionSpec as P

AZ = 1024
RG = 2048
TAPS = 8
WIN_AZ = 11
SPAN = 2
PARTS = 16
LINES = AZ // PARTS
COLS = RG // PARTS
ROWS = LINES + 16
PULSE = RG // 2
WIDE = 256
DEPTH = PULSE + WIDE
PAD = 128

two_pi = 2.0 * math.pi
epsilon = 1e-06
f32 = jnp.float32
bf16 = jnp.bfloat16


def mini_dft():
    first = np.arange(PARTS).reshape(PARTS, 1, 1)
    second = np.arange(LINES).reshape(1, LINES, 1)
    line = np.arange(LINES).reshape(1, 1, LINES)
    angle = two_pi * (((first + PARTS * second) * line) % AZ) / AZ
    real, imag = np.cos(angle) / 32.0, -np.sin(angle) / 32.0
    forward = np.concatenate(
        [np.concatenate([real, -imag], 2), np.concatenate([imag, real], 2)], 1
    )
    return forward, forward.transpose(0, 2, 1)


def fft_of(terms, sign):
    count = len(terms)
    if count == 1:
        return terms
    even, odd = fft_of(terms[::2], sign), fft_of(terms[1::2], sign)
    low, high = [], []
    for k in range(count // 2):
        re, im = odd[k]
        if k == 0:
            turned = (re, im)
        elif 4 * k == count:
            turned = (-im, re) if sign > 0 else (im, -re)
        else:
            c, s = math.cos(two_pi * k / count), sign * math.sin(two_pi * k / count)
            turned = (re * c - im * s, re * s + im * c)
        low.append((even[k][0] + turned[0], even[k][1] + turned[1]))
        high.append((even[k][0] - turned[0], even[k][1] - turned[1]))
    return low + high


def chirp_table(rate, table):
    lane = lax.broadcasted_iota(jnp.int32, (8, 2 * WIDE), 1)
    for part in range(DEPTH // WIDE):
        lag = WIDE * part - jnp.where(lane < WIDE, lane, lane - 2 * WIDE)
        inside = (lag >= 0) & (lag < PULSE)
        offset = (lag.astype(f32) - 0.5 * PULSE) / PULSE
        phase = math.pi * PULSE * rate * offset * offset
        amplitude = 1.0 / math.sqrt(PULSE)
        values = (
            jnp.where(inside, jnp.cos(phase) * amplitude, 0.0),
            jnp.where(inside, -jnp.sin(phase) * amplitude, 0.0),
        )
        for which, value in enumerate(values):
            spread = jnp.broadcast_to(value[0:1], (WIDE, 2 * WIDE))
            rolled = pltpu.roll(spread, 0, 1, stride=1, stride_axis=0)
            table[WIDE * part : WIDE * (part + 1), WIDE * which : WIDE * (which + 1)] = rolled[
                :, :WIDE
            ].astype(bf16)


def azimuth_filter(rate_row, shift_re, shift_im, filt):
    row = lax.broadcasted_iota(jnp.int32, (LINES, COLS), 0)

    def one_residue(first, carry):
        freq = first + PARTS * row
        centered = ((freq + AZ // 2) % AZ - AZ // 2).astype(f32) / AZ
        phase = math.pi * AZ * rate_row * centered * centered
        re, im = jnp.cos(phase), jnp.sin(phase)
        sre, sim = shift_re[first], shift_im[first]
        filt[first, :LINES] = re * sre - im * sim
        filt[first, LINES:] = re * sim + im * sre
        return carry

    lax.fori_loop(0, PARTS, one_residue, 0)


def azimuth_focus(columns, filt, forward, backward, work, planes, out_ref):
    step = 16

    def spread_lines(chunk, carry):
        rows = pl.ds(pl.multiple_of(chunk * step, step), step)
        terms = [
            (columns[j, 0, rows].astype(f32), columns[j, 1, rows].astype(f32)) for j in range(PARTS)
        ]
        lower = pl.ds(pl.multiple_of(chunk * step + LINES, step), step)
        for first, (re, im) in enumerate(fft_of(terms, -1)):
            work[first, rows] = re.astype(bf16)
            work[first, lower] = im.astype(bf16)
        return carry

    lax.fori_loop(0, LINES // step, spread_lines, 0)

    def one_residue(first, carry):
        spectrum = jnp.dot(forward[first], work[first], preferred_element_type=f32)
        re, im = spectrum[:LINES], spectrum[LINES:]
        gre, gim = filt[first, :LINES], filt[first, LINES:]
        filtered = jnp.concatenate([re * gre - im * gim, re * gim + im * gre], 0).astype(bf16)
        planes[first] = jnp.dot(backward[first], filtered, preferred_element_type=f32)
        return carry

    lax.fori_loop(0, PARTS, one_residue, 0)

    def gather_lines(chunk, carry):
        rows = pl.ds(pl.multiple_of(chunk * step, step), step)
        lower = pl.ds(pl.multiple_of(chunk * step + LINES, step), step)
        terms = [(planes[first, rows], planes[first, lower]) for first in range(PARTS)]
        for j, (re, im) in enumerate(fft_of(terms, 1)):
            out_ref[j, 0, rows] = re.astype(bf16)
            out_ref[j, 1, rows] = im.astype(bf16)
        return carry

    lax.fori_loop(0, LINES // step, gather_lines, 0)

    for part in range(2):
        zero = jnp.zeros((8, COLS), f32)
        for j in range(PARTS):
            below = out_ref[j - 1, part, 48:64].astype(f32)[8:] if j > 0 else zero
            above = out_ref[j + 1, part, 0:16].astype(f32)[:8] if j < PARTS - 1 else zero
            out_ref[j, part, LINES:ROWS] = jnp.concatenate([below, above], 0).astype(bf16)


MESH = pl.DeviceIdType.MESH
HALF = 16


class Place:
    def __init__(self):
        self.date, self.swath = lax.axis_index("date"), lax.axis_index("swath")
        self.side, self.spot = self.date // HALF, self.date % HALF
        chip, self.core = self.swath // 2, self.swath % 2
        self.end, self.rank = chip // 4, chip % 4

    def chip(self, turn):
        far = turn // 4
        return 4 * ((self.end + 1 + far) % 2) + (self.rank + turn + far) % 4

    def arrival(self, turn):
        return 2 * self.chip((turn // 2 + 7) % 8) + (self.core + turn % 2) % 2

    def departure(self, turn):
        return 2 * self.chip(turn // 2) + (self.core + 1 + turn % 2) % 2


def send(source, target, leaves, lands, date, swath):
    pltpu.make_async_remote_copy(
        source, target, leaves, lands, device_id=(date, swath), device_id_type=MESH
    ).start()


def drain(block, sem):
    pltpu.make_async_copy(block, block, sem).wait()


def greet(place):
    barrier = pltpu.get_barrier_semaphore()
    first = HALF * place.side

    def tell(date, swath):
        pl.semaphore_signal(barrier, inc=1, device_id=(date, swath), device_id_type=MESH)

    def each(turn, carry):
        tell(place.date, (place.swath + turn) % PARTS)
        return carry

    lax.fori_loop(1, PARTS, each, 0)

    @pl.when(place.spot != HALF - 1)
    def _():
        tell(place.date + 1, place.swath)

    for q in range(2):
        tell(HALF * (1 - place.side) + q, place.spot)

    @pl.when(place.spot >= HALF - 2)
    def _():
        def every(turn, carry):
            tell(first + (place.spot + turn) % HALF, place.swath)
            return carry

        lax.fori_loop(1, HALF, every, 0)

    wanted = (
        (PARTS - 1)
        + jnp.where(place.spot != 0, 1, 0)
        + jnp.where(place.spot <= 1, PARTS, 0)
        + jnp.where(place.spot != HALF - 1, 1, 0)
        + jnp.where(place.spot != HALF - 2, 1, 0)
    )
    pl.semaphore_wait(barrier, wanted)


def focus_kernel(
    rate_ref,
    echo_ref,
    rate_row,
    shift_re,
    shift_im,
    forward,
    backward,
    own,
    following,
    after,
    table,
    extended,
    leaving,
    columns,
    filt,
    work,
    planes,
    blocks,
    crossing,
    turn_send,
    turn_recv,
    back_send,
    back_recv,
    wrap_send,
    wrap_recv,
    next_send,
    next_recv,
    last_send,
    last_recv,
    tail_send,
):
    place = Place()
    chirp_table(rate_ref[0], table)
    for part in range(2):
        rows = slice(LINES * part, LINES * (part + 1))
        extended[rows, :RG] = echo_ref[part]
        extended[rows, RG:] = echo_ref[part, :, :PULSE]
    greet(place)

    def one_block(turn, carry):
        block = place.chip(turn)
        window = extended[:, pl.ds(pl.multiple_of(block * WIDE, WIDE), DEPTH)]
        product = jnp.dot(window, table[...], preferred_element_type=f32)
        real = product[:LINES, :WIDE] - product[LINES:, WIDE:]
        imag = product[:LINES, WIDE:] + product[LINES:, :WIDE]
        for half in range(2):
            cols = slice(COLS * half, COLS * (half + 1))
            leaving[2 * block + half, 0] = real[:, cols].astype(bf16)
            leaving[2 * block + half, 1] = imag[:, cols].astype(bf16)
        for half in range(2):
            goal = 2 * block + (place.core + 1 + half) % 2

            @pl.when(goal != place.swath)
            def _():
                send(
                    leaving.at[goal],
                    columns.at[place.swath],
                    turn_send,
                    turn_recv,
                    place.date,
                    goal,
                )

            @pl.when(goal == place.swath)
            def _():
                pltpu.make_async_copy(leaving.at[goal], columns.at[goal], turn_recv).start()

        return carry

    lax.fori_loop(0, RG // WIDE, one_block, 0)
    azimuth_filter(rate_row[...], shift_re, shift_im, filt)
    drain(columns, turn_recv)
    drain(leaving.at[pl.ds(0, PARTS - 1)], turn_send)

    azimuth_focus(columns, filt, forward, backward, work, planes, blocks)

    leads = place.spot <= 1
    other = HALF * (1 - place.side)

    def hand_back(turn, carry):
        goal = place.departure(turn)

        @pl.when(leads)
        def _():
            lane = place.spot % 2
            send(
                blocks.at[goal],
                crossing.at[lane],
                wrap_send,
                wrap_recv.at[lane],
                other + place.swath,
                goal,
            )

        @pl.when(goal != place.swath)
        def _():
            send(
                blocks.at[goal],
                own.at[place.swath],
                back_send,
                back_recv.at[place.swath],
                place.date,
                goal,
            )

        @pl.when(goal == place.swath)
        def _():
            pltpu.make_async_copy(blocks.at[goal], own.at[goal], back_recv.at[goal]).start()

        return carry

    lax.fori_loop(0, PARTS, hand_back, 0)

    has_next = place.spot != HALF - 1
    has_back = place.spot != 0
    delay = 2

    def pass_on(turn, carry):
        @pl.when(turn < PARTS)
        def _():
            piece = place.arrival(turn % PARTS)
            drain(own.at[piece], back_recv.at[piece])

            @pl.when(has_back)
            def _():
                send(
                    own.at[piece],
                    following.at[piece],
                    next_send,
                    next_recv.at[piece],
                    place.date - 1,
                    place.swath,
                )

        @pl.when((turn >= delay) & has_next)
        def _():
            piece = place.arrival((turn + PARTS - delay) % PARTS)
            drain(following.at[piece], next_recv.at[piece])

            @pl.when(has_back)
            def _():
                send(
                    following.at[piece],
                    after.at[piece],
                    last_send,
                    last_recv,
                    place.date - 1,
                    place.swath,
                )

        return carry

    lax.fori_loop(0, PARTS + delay, pass_on, 0)

    for lane in range(2):
        drain(crossing.at[lane], wrap_recv.at[lane])
    spot = place.spot
    deliveries = (
        (0, following, next_recv.at[spot], HALF - 1),
        (1, after, last_recv, HALF - 1),
        (0, after, last_recv, HALF - 2),
    )
    for index, (lane, target, lands, goal) in enumerate(deliveries):

        @pl.when(spot != goal)
        def _():
            send(
                crossing.at[lane],
                target.at[spot],
                tail_send.at[index],
                lands,
                HALF * place.side + goal,
                place.swath,
            )

        @pl.when(spot == goal)
        def _():
            pltpu.make_async_copy(crossing.at[lane], target.at[spot], lands).start()

    @pl.when(spot == HALF - 1)
    def _():
        def arrive(piece, carry):
            drain(following.at[piece], next_recv.at[piece])
            return carry

        lax.fori_loop(0, PARTS, arrive, 0)

    drain(after, last_recv)
    drain(blocks.at[pl.ds(0, PARTS - 1)], back_send)

    @pl.when(leads)
    def _():
        drain(blocks, wrap_send)

    @pl.when(has_back)
    def _():
        drain(own, next_send)

    @pl.when(has_back & has_next)
    def _():
        drain(following, last_send)

    for index, (lane, target, lands, goal) in enumerate(deliveries):

        @pl.when(spot != goal)
        def _():
            drain(crossing.at[lane], tail_send.at[index])


def shift_response(frac, offset):
    half_taps = TAPS // 2
    position = jnp.arange(TAPS, dtype=jnp.int32).astype(f32) - (half_taps - 1) - frac
    taps = jnp.sinc(position) * (0.5 + 0.5 * jnp.cos(math.pi * position / half_taps))
    freq = jnp.arange(PARTS)[:, None] + PARTS * jnp.arange(LINES)[None, :]
    real, imag = 0.0, 0.0
    for tap in range(TAPS):
        angle = (freq * (offset + tap) % AZ).astype(f32) * (two_pi / AZ)
        real = real + taps[tap] * jnp.cos(angle)
        imag = imag + taps[tap] * jnp.sin(angle)
    spread = (PARTS, LINES, COLS)
    return (
        jnp.broadcast_to(real[:, :, None], spread),
        jnp.broadcast_to(imag[:, :, None], spread),
    )


def line_sums():
    line = np.arange(LINES)[:, None]
    row = np.arange(ROWS)[None, :]
    place = np.where(row < LINES, row, np.where(row < LINES + 8, row - LINES - 8, row - 8))
    return (np.abs(place - line) <= WIN_AZ // 2).astype(np.float32)


def coherence_kernel(sums_ref, own_ref, next_ref, after_ref, image_ref, result_ref, held):
    edge = jnp.zeros((7, LINES, PAD), f32)
    held[:, :, :PAD] = edge
    held[:, :, PAD + RG :] = edge
    sums = sums_ref[...]

    def one_piece(piece, carry):
        are, aim = own_ref[piece, 0].astype(f32), own_ref[piece, 1].astype(f32)
        maps = [are * are + aim * aim]
        for other in (next_ref, after_ref):
            bre, bim = other[piece, 0].astype(f32), other[piece, 1].astype(f32)
            maps += [bre * bre + bim * bim, are * bre + aim * bim, aim * bre - are * bim]
        lanes = pl.ds(pl.multiple_of(piece * COLS, COLS), COLS)
        stacked = jnp.concatenate([m.astype(bf16) for m in maps], 1)
        summed = jnp.dot(sums, stacked, preferred_element_type=f32)
        inner = pl.ds(pl.multiple_of(piece * COLS + PAD, COLS), COLS)
        for which in range(7):
            held[which, :, inner] = summed[:, COLS * which : COLS * (which + 1)]
        for part in range(2):
            image_ref[0, part, :, lanes] = own_ref[piece, part, :LINES]
        return carry

    lax.fori_loop(0, PARTS, one_piece, 0)

    def one_chunk(chunk, carry):
        rows = pl.ds(pl.multiple_of(chunk * 16, 16), 16)
        width = RG + 2 * PAD

        def across(which):
            value = held[which, rows]
            near = pltpu.roll(value, 1, 1) + pltpu.roll(value, width - 1, 1)
            far = pltpu.roll(value, 2, 1) + pltpu.roll(value, width - 2, 1)
            return (value + near + far)[:, PAD : PAD + RG]

        own_power = across(0)
        for pair in range(SPAN):
            scale = lax.rsqrt(own_power * across(3 * pair + 1) + epsilon)
            for part in range(2):
                term = across(3 * pair + 2 + part) * scale
                result_ref[0, pair, part, rows] = term.astype(bf16)
        return carry

    lax.fori_loop(0, LINES // 16, one_chunk, 0)


def vmem(count):
    return [pl.BlockSpec(memory_space=pltpu.VMEM)] * count


def params(**more):
    return pltpu.CompilerParams(vmem_limit_bytes=56 * 1024 * 1024, **more)


def coherence_call(own, following, after):
    return pl.pallas_call(
        coherence_kernel,
        out_shape=(
            jax.ShapeDtypeStruct((1, 2, LINES, RG), bf16),
            jax.ShapeDtypeStruct((1, SPAN, 2, LINES, RG), bf16),
        ),
        in_specs=vmem(4),
        out_specs=tuple(vmem(2)),
        scratch_shapes=[pltpu.VMEM((7, LINES, RG + 2 * PAD), f32)],
        compiler_params=params(),
    )(jnp.asarray(line_sums(), bf16), own, following, after)


def focus_call(raw_echo, range_rate, azimuth_rate, line_offset, frac_shift):
    shift_re, shift_im = shift_response(frac_shift[0], line_offset[0])
    forward, backward = mini_dft()
    dma = pltpu.SemaphoreType.DMA
    return pl.pallas_call(
        focus_kernel,
        out_shape=(jax.ShapeDtypeStruct((PARTS, 2, ROWS, COLS), bf16),) * 3,
        in_specs=[pl.BlockSpec(memory_space=pltpu.SMEM)] + vmem(6),
        out_specs=tuple(vmem(3)),
        scratch_shapes=[
            pltpu.VMEM((DEPTH, 2 * WIDE), bf16),
            pltpu.VMEM((2 * LINES, RG + PULSE), bf16),
            pltpu.VMEM((PARTS, 2, LINES, COLS), bf16),
            pltpu.VMEM((PARTS, 2, LINES, COLS), bf16),
            pltpu.VMEM((PARTS, 2 * LINES, COLS), f32),
            pltpu.VMEM((PARTS, 2 * LINES, COLS), bf16),
            pltpu.VMEM((PARTS, 2 * LINES, COLS), f32),
            pltpu.VMEM((PARTS, 2, ROWS, COLS), bf16),
            pltpu.VMEM((2, 2, ROWS, COLS), bf16),
            dma,
            dma,
            dma,
            dma((PARTS,)),
            dma,
            dma((2,)),
            dma,
            dma((PARTS,)),
            dma,
            dma,
            dma((3,)),
        ],
        compiler_params=params(collective_id=0, has_side_effects=True),
    )(
        range_rate.reshape(1),
        raw_echo[0],
        azimuth_rate.reshape(1, COLS),
        shift_re,
        shift_im,
        jnp.asarray(forward, bf16),
        jnp.asarray(backward, bf16),
    )


def body(raw_echo, range_rate, azimuth_rate, line_offset, frac_shift):
    return coherence_call(
        *focus_call(raw_echo, range_rate, azimuth_rate, line_offset, frac_shift)
    )


def solution(mesh):
    placed = (P("date", None, "swath", None), P(), P("swath"), P("date"), P("date"))
    return jax.shard_map(
        body,
        mesh=mesh,
        in_specs=placed,
        out_specs=(P("date", None, "swath", None), P("date", None, None, "swath", None)),
        check_vma=False,
    )
```

```python
import functools
import math

import numpy as np
import jax
import jax.numpy as jnp
from jax import lax
from jax.experimental import pallas as pl
from jax.experimental.pallas import tpu as pltpu
from jax.sharding import PartitionSpec as P

AZ = 1024
RG = 2048
TAPS = 8
WIN_AZ = 11
WIN_RG = 5
SPAN = 2
PARTS = 16
LINES = AZ // PARTS
COLS = RG // PARTS
ROWS = LINES + 16
PULSE = RG // 2
WIDE = 256
DEPTH = PULSE + WIDE
PAD = 128

two_pi = 2.0 * math.pi
epsilon = 1e-06
f32 = jnp.float32
bf16 = jnp.bfloat16


def mini_dft():
    first = np.arange(PARTS).reshape(PARTS, 1, 1)
    second = np.arange(LINES).reshape(1, LINES, 1)
    line = np.arange(LINES).reshape(1, 1, LINES)
    angle = two_pi * (((first + PARTS * second) * line) % AZ) / AZ
    real, imag = np.cos(angle) / 32.0, -np.sin(angle) / 32.0
    forward = np.concatenate(
        [np.concatenate([real, -imag], 2), np.concatenate([imag, real], 2)], 1
    )
    return forward, forward.transpose(0, 2, 1)


def fft_of(terms, sign):
    count = len(terms)
    if count == 1:
        return terms
    even, odd = fft_of(terms[::2], sign), fft_of(terms[1::2], sign)
    low, high = [], []
    for k in range(count // 2):
        re, im = odd[k]
        if k == 0:
            turned = (re, im)
        elif 4 * k == count:
            turned = (-im, re) if sign > 0 else (im, -re)
        else:
            c, s = math.cos(two_pi * k / count), sign * math.sin(two_pi * k / count)
            turned = (re * c - im * s, re * s + im * c)
        low.append((even[k][0] + turned[0], even[k][1] + turned[1]))
        high.append((even[k][0] - turned[0], even[k][1] - turned[1]))
    return low + high


def chirp_table(rate, table):
    lane = lax.broadcasted_iota(jnp.int32, (8, 2 * WIDE), 1)
    for part in range(DEPTH // WIDE):
        lag = WIDE * part - jnp.where(lane < WIDE, lane, lane - 2 * WIDE)
        inside = (lag >= 0) & (lag < PULSE)
        offset = (lag.astype(f32) - 0.5 * PULSE) / PULSE
        phase = math.pi * PULSE * rate * offset * offset
        amplitude = 1.0 / math.sqrt(PULSE)
        values = (
            jnp.where(inside, jnp.cos(phase) * amplitude, 0.0),
            jnp.where(inside, -jnp.sin(phase) * amplitude, 0.0),
        )
        for which, value in enumerate(values):
            spread = jnp.broadcast_to(value[0:1], (WIDE, 2 * WIDE))
            rolled = pltpu.roll(spread, 0, 1, stride=1, stride_axis=0)
            table[WIDE * part : WIDE * (part + 1), WIDE * which : WIDE * (which + 1)] = rolled[
                :, :WIDE
            ].astype(bf16)


def azimuth_filter(rate_row, frac, offset, filt):
    row = lax.broadcasted_iota(jnp.int32, (LINES, COLS), 0)
    half_taps = TAPS // 2
    tap_id = lax.broadcasted_iota(jnp.int32, (TAPS, COLS), 0)
    position = tap_id.astype(f32) - (half_taps - 1) - frac
    middle = position == 0.0
    turned = jnp.where(middle, 1.0, math.pi * position)
    taps = jnp.where(middle, 1.0, jnp.sin(turned) / turned)
    taps = taps * (0.5 + 0.5 * jnp.cos(math.pi * position / half_taps))
    base = row.astype(f32) * (two_pi / LINES)
    step_re, step_im = math.cos(two_pi / AZ), math.sin(two_pi / AZ)

    def one_residue(first, carry):
        zre, zim = carry
        freq = first + PARTS * row
        centered = ((freq + AZ // 2) % AZ - AZ // 2).astype(f32) / AZ
        start = ((freq * offset) % AZ).astype(f32) * (two_pi / AZ)
        phase = math.pi * AZ * rate_row * centered * centered
        re, im = jnp.cos(phase), jnp.sin(phase)
        sre, sim = jnp.cos(start), jnp.sin(start)
        re, im = re * sre - im * sim, re * sim + im * sre
        hre = jnp.broadcast_to(taps[TAPS - 1 : TAPS], (LINES, COLS))
        him = jnp.zeros((LINES, COLS), f32)
        for tap in range(TAPS - 2, -1, -1):
            hre, him = hre * zre - him * zim + taps[tap : tap + 1], hre * zim + him * zre
        filt[first, :LINES] = re * hre - im * him
        filt[first, LINES:] = re * him + im * hre
        return (zre * step_re - zim * step_im, zre * step_im + zim * step_re)

    lax.fori_loop(0, PARTS, one_residue, (jnp.cos(base), jnp.sin(base)))


def azimuth_focus(columns, filt, forward, backward, work, planes, out_ref):
    step = 16

    def spread_lines(chunk, carry):
        rows = pl.ds(pl.multiple_of(chunk * step, step), step)
        terms = [
            (columns[j, 0, rows].astype(f32), columns[j, 1, rows].astype(f32)) for j in range(PARTS)
        ]
        lower = pl.ds(pl.multiple_of(chunk * step + LINES, step), step)
        for first, (re, im) in enumerate(fft_of(terms, -1)):
            work[first, rows] = re.astype(bf16)
            work[first, lower] = im.astype(bf16)
        return carry

    lax.fori_loop(0, LINES // step, spread_lines, 0)

    def one_residue(first, carry):
        spectrum = jnp.dot(forward[first], work[first], preferred_element_type=f32)
        re, im = spectrum[:LINES], spectrum[LINES:]
        gre, gim = filt[first, :LINES], filt[first, LINES:]
        filtered = jnp.concatenate([re * gre - im * gim, re * gim + im * gre], 0).astype(bf16)
        planes[first] = jnp.dot(backward[first], filtered, preferred_element_type=f32)
        return carry

    lax.fori_loop(0, PARTS, one_residue, 0)

    def gather_lines(chunk, carry):
        rows = pl.ds(pl.multiple_of(chunk * step, step), step)
        lower = pl.ds(pl.multiple_of(chunk * step + LINES, step), step)
        terms = [(planes[first, rows], planes[first, lower]) for first in range(PARTS)]
        for j, (re, im) in enumerate(fft_of(terms, 1)):
            out_ref[j, 0, rows] = re.astype(bf16)
            out_ref[j, 1, rows] = im.astype(bf16)
        return carry

    lax.fori_loop(0, LINES // step, gather_lines, 0)

    for part in range(2):
        zero = jnp.zeros((8, COLS), f32)
        for j in range(PARTS):
            below = out_ref[j - 1, part, 48:64].astype(f32)[8:] if j > 0 else zero
            above = out_ref[j + 1, part, 0:16].astype(f32)[:8] if j < PARTS - 1 else zero
            out_ref[j, part, LINES:ROWS] = jnp.concatenate([below, above], 0).astype(bf16)


MESH = pl.DeviceIdType.MESH
HALF = 16


class Place:
    def __init__(self):
        self.date, self.swath = lax.axis_index("date"), lax.axis_index("swath")
        self.side, self.spot = self.date // HALF, self.date % HALF

    def departure(self, turn):
        return (self.swath + 1 + turn) % PARTS

    def arrival(self, turn):
        return (self.swath + PARTS - turn) % PARTS


def send(source, target, leaves, lands, date, swath):
    pltpu.make_async_remote_copy(
        source, target, leaves, lands, device_id=(date, swath), device_id_type=MESH
    ).start()


def drain(block, sem):
    pltpu.make_async_copy(block, block, sem).wait()


def tell(date, swath):
    barrier = pltpu.get_barrier_semaphore()
    pl.semaphore_signal(barrier, inc=1, device_id=(date, swath), device_id_type=MESH)


def greet(place):
    def each(turn, carry):
        tell(place.date, (place.swath + turn) % PARTS)
        return carry

    lax.fori_loop(1, PARTS, each, 0)

    @pl.when(place.spot != HALF - 1)
    def _():
        tell(place.date + 1, place.swath)

    for lane in range(2):

        @pl.when(place.spot != lane)
        def _():
            tell(HALF * place.side + lane, place.swath)

    @pl.when(place.spot == HALF - 1)
    def _():
        def every(part, carry):
            tell(HALF * (1 - place.side) + (place.swath + part) % HALF, part)
            return carry

        lax.fori_loop(0, PARTS, every, 0)


def await_greetings(place):
    wanted = (
        PARTS
        + jnp.where(place.spot != 0, 1, 0)
        + jnp.where(place.spot <= 1, HALF - 1, 0)
    )
    pl.semaphore_wait(pltpu.get_barrier_semaphore(), wanted)


def focus_kernel(
    rate_ref,
    offset_ref,
    frac_ref,
    echo_ref,
    rate_row,
    forward,
    backward,
    own,
    following,
    after,
    table,
    extended,
    leaving,
    columns,
    filt,
    work,
    planes,
    blocks,
    crossing,
    turn_send,
    turn_recv,
    back_send,
    back_recv,
    wrap_send,
    wrap_recv,
    next_send,
    next_recv,
    last_send,
    last_recv,
    tail_send,
):
    place = Place()
    greet(place)
    chirp_table(rate_ref[0], table)
    for part in range(2):
        rows = slice(LINES * part, LINES * (part + 1))
        extended[rows, :RG] = echo_ref[part]
        extended[rows, RG:] = echo_ref[part, :, :PULSE]

    def one_block(block, carry):
        window = extended[:, pl.ds(pl.multiple_of(block * WIDE, WIDE), DEPTH)]
        product = jnp.dot(window, table[...], preferred_element_type=f32)
        real = product[:LINES, :WIDE] - product[LINES:, WIDE:]
        imag = product[:LINES, WIDE:] + product[LINES:, :WIDE]
        for half in range(2):
            cols = slice(COLS * half, COLS * (half + 1))
            leaving[2 * block + half, 0] = real[:, cols].astype(bf16)
            leaving[2 * block + half, 1] = imag[:, cols].astype(bf16)
        return carry

    lax.fori_loop(0, RG // WIDE, one_block, 0)
    await_greetings(place)

    def hand_over(turn, carry):
        goal = place.departure(turn)
        send(leaving.at[goal], columns.at[place.swath], turn_send, turn_recv, place.date, goal)
        return carry

    lax.fori_loop(0, PARTS - 1, hand_over, 0)
    kept = leaving.at[place.swath]
    pltpu.make_async_copy(kept, columns.at[place.swath], turn_recv).start()
    azimuth_filter(rate_row[...], frac_ref[0], offset_ref[0], filt)
    drain(columns, turn_recv)
    drain(leaving.at[pl.ds(0, PARTS - 1)], turn_send)

    azimuth_focus(columns, filt, forward, backward, work, planes, blocks)

    side, spot, date, swath = place.side, place.spot, place.date, place.swath
    leads = spot <= 1
    lane = spot % 2

    @pl.when(leads)
    def _():
        def scatter(part, carry):
            goal = (swath + part) % HALF

            @pl.when(goal != spot)
            def _():
                send(
                    blocks.at[part],
                    crossing.at[lane],
                    wrap_send,
                    wrap_recv.at[lane],
                    HALF * side + goal,
                    swath,
                )

            @pl.when(goal == spot)
            def _():
                pltpu.make_async_copy(
                    blocks.at[part], crossing.at[lane], wrap_recv.at[lane]
                ).start()

            return carry

        lax.fori_loop(0, PARTS, scatter, 0)

    def hand_back(turn, carry):
        goal = place.departure(turn)
        send(blocks.at[goal], own.at[swath], back_send, back_recv.at[swath], date, goal)
        return carry

    lax.fori_loop(0, PARTS - 1, hand_back, 0)
    pltpu.make_async_copy(blocks.at[swath], own.at[swath], back_recv.at[swath]).start()

    for which, target, lands in ((0, following, next_recv.at[swath]), (1, after, last_recv)):
        drain(crossing.at[which], wrap_recv.at[which])
        send(
            crossing.at[which],
            target.at[swath],
            tail_send.at[which],
            lands,
            HALF * (1 - side) + HALF - 1,
            (spot + HALF - swath) % HALF,
        )

    has_next = spot != HALF - 1
    has_back = spot != 0
    delay = 2

    def relay(piece):
        drain(following.at[piece], next_recv.at[piece])

        @pl.when(has_back)
        def _():
            send(following.at[piece], after.at[piece], last_send, last_recv, date - 1, swath)

    def pass_on(turn, carry):
        @pl.when(turn < PARTS)
        def _():
            piece = place.arrival(turn % PARTS)
            drain(own.at[piece], back_recv.at[piece])

            @pl.when(has_back)
            def _():
                send(
                    own.at[piece],
                    following.at[piece],
                    next_send,
                    next_recv.at[piece],
                    date - 1,
                    swath,
                )

        @pl.when((turn >= delay) & has_next)
        def _():
            relay(place.arrival((turn + PARTS - delay) % PARTS))

        return carry

    lax.fori_loop(0, PARTS + delay, pass_on, 0)

    @pl.when(spot == HALF - 1)
    def _():
        def late(turn, carry):
            relay(place.arrival(turn))
            return carry

        lax.fori_loop(0, PARTS, late, 0)

    drain(after, last_recv)
    drain(blocks.at[pl.ds(0, PARTS - 1)], back_send)

    @pl.when(leads)
    def _():
        drain(blocks.at[pl.ds(0, HALF - 1)], wrap_send)

    @pl.when(has_back)
    def _():
        drain(own, next_send)
        drain(following, last_send)

    for which in range(2):
        drain(crossing.at[which], tail_send.at[which])


def line_sums():
    line = np.arange(LINES)[:, None]
    row = np.arange(ROWS)[None, :]
    place = np.where(row < LINES, row, np.where(row < LINES + 8, row - LINES - 8, row - 8))
    return (np.abs(place - line) <= WIN_AZ // 2).astype(np.float32)


def sample_sums():
    sample = np.arange(2 * WIDE)[:, None]
    middle = np.arange(WIDE)[None, :] + PAD
    return (np.abs(sample - middle) <= WIN_RG // 2).astype(np.float32)


def coherence_kernel(
    lines_ref, samples_ref, own_ref, next_ref, after_ref, image_ref, result_ref, held
):
    edge = jnp.zeros((7 * LINES, PAD), bf16)
    held[:, :PAD] = edge
    held[:, PAD + RG :] = edge
    sums = lines_ref[...]

    def one_piece(piece, carry):
        are, aim = own_ref[piece, 0].astype(f32), own_ref[piece, 1].astype(f32)
        maps = [are * are + aim * aim]
        for other in (next_ref, after_ref):
            bre, bim = other[piece, 0].astype(f32), other[piece, 1].astype(f32)
            maps += [bre * bre + bim * bim, are * bre + aim * bim, aim * bre - are * bim]
        lanes = pl.ds(pl.multiple_of(piece * COLS, COLS), COLS)
        stacked = jnp.concatenate([m.astype(bf16) for m in maps], 1)
        summed = jnp.dot(sums, stacked, preferred_element_type=f32)
        inner = pl.ds(pl.multiple_of(piece * COLS + PAD, COLS), COLS)
        for which in range(7):
            held[LINES * which : LINES * (which + 1), inner] = summed[
                :, COLS * which : COLS * (which + 1)
            ].astype(bf16)
        for part in range(2):
            image_ref[0, part, :, lanes] = own_ref[piece, part, :LINES]
        return carry

    lax.fori_loop(0, PARTS, one_piece, 0)

    def one_span(span, carry):
        start = pl.multiple_of(span * WIDE, WIDE)
        window = held[:, pl.ds(start, 2 * WIDE)]
        boxes = jnp.dot(window, samples_ref[...], preferred_element_type=f32)
        box = [boxes[LINES * which : LINES * (which + 1)] for which in range(7)]
        for pair in range(SPAN):
            scale = lax.rsqrt(box[0] * box[3 * pair + 1] + epsilon)
            for part in range(2):
                term = box[3 * pair + 2 + part] * scale
                result_ref[0, pair, part, :, pl.ds(start, WIDE)] = term.astype(bf16)
        return carry

    lax.fori_loop(0, RG // WIDE, one_span, 0)


def vmem(count):
    return [pl.BlockSpec(memory_space=pltpu.VMEM)] * count


def params(**more):
    return pltpu.CompilerParams(vmem_limit_bytes=56 * 1024 * 1024, **more)


def coherence_call(own, following, after):
    return pl.pallas_call(
        coherence_kernel,
        out_shape=(
            jax.ShapeDtypeStruct((1, 2, LINES, RG), bf16),
            jax.ShapeDtypeStruct((1, SPAN, 2, LINES, RG), bf16),
        ),
        in_specs=vmem(5),
        out_specs=tuple(vmem(2)),
        scratch_shapes=[pltpu.VMEM((7 * LINES, RG + 2 * PAD), bf16)],
        compiler_params=params(),
    )(
        jnp.asarray(line_sums(), bf16),
        jnp.asarray(sample_sums(), bf16),
        own,
        following,
        after,
    )


def focus_call(raw_echo, range_rate, azimuth_rate, line_offset, frac_shift):
    forward, backward = mini_dft()
    dma = pltpu.SemaphoreType.DMA
    return pl.pallas_call(
        focus_kernel,
        out_shape=(jax.ShapeDtypeStruct((PARTS, 2, ROWS, COLS), bf16),) * 3,
        in_specs=[pl.BlockSpec(memory_space=pltpu.SMEM)] * 3 + vmem(4),
        out_specs=tuple(vmem(3)),
        scratch_shapes=[
            pltpu.VMEM((DEPTH, 2 * WIDE), bf16),
            pltpu.VMEM((2 * LINES, RG + PULSE), bf16),
            pltpu.VMEM((PARTS, 2, LINES, COLS), bf16),
            pltpu.VMEM((PARTS, 2, LINES, COLS), bf16),
            pltpu.VMEM((PARTS, 2 * LINES, COLS), f32),
            pltpu.VMEM((PARTS, 2 * LINES, COLS), bf16),
            pltpu.VMEM((PARTS, 2 * LINES, COLS), f32),
            pltpu.VMEM((PARTS, 2, ROWS, COLS), bf16),
            pltpu.VMEM((2, 2, ROWS, COLS), bf16),
            dma,
            dma,
            dma,
            dma((PARTS,)),
            dma,
            dma((2,)),
            dma,
            dma((PARTS,)),
            dma,
            dma,
            dma((2,)),
        ],
        compiler_params=params(collective_id=0, has_side_effects=True),
    )(
        range_rate.reshape(1),
        line_offset,
        frac_shift,
        raw_echo[0],
        azimuth_rate.reshape(1, COLS),
        jnp.asarray(forward, bf16),
        jnp.asarray(backward, bf16),
    )


def body(raw_echo, range_rate, azimuth_rate, line_offset, frac_shift):
    return coherence_call(
        *focus_call(raw_echo, range_rate, azimuth_rate, line_offset, frac_shift)
    )


def solution(mesh):
    placed = (P("date", None, "swath", None), P(), P("swath"), P("date"), P("date"))
    return jax.shard_map(
        body,
        mesh=mesh,
        in_specs=placed,
        out_specs=(P("date", None, "swath", None), P("date", None, None, "swath", None)),
        check_vma=False,
    )
```

```python
import functools
import math

import numpy as np
import jax
import jax.numpy as jnp
from jax import lax
from jax.experimental import pallas as pl
from jax.experimental.pallas import tpu as pltpu
from jax.sharding import PartitionSpec as P

AZ = 1024
RG = 2048
TAPS = 8
WIN_AZ = 11
WIN_RG = 5
SPAN = 2
PARTS = 16
LINES = AZ // PARTS
COLS = RG // PARTS
ROWS = LINES + 16
TILE = 16
WAVES = LINES // TILE
ORDER = (0, WAVES - 1) + tuple(range(1, WAVES - 1))
STRIDES = (8, 7, 4, 1, 15, 9, 10, 5, 2, 14, 6, 11, 12, 3, 13)
AHEAD = 5
PULSE = RG // 2
WIDE = 256
DEPTH = PULSE + WIDE
PAD = 128

two_pi = 2.0 * math.pi
epsilon = 1e-06
f32 = jnp.float32
bf16 = jnp.bfloat16


def mini_dft():
    first = np.arange(PARTS).reshape(PARTS, 1, 1)
    second = np.arange(LINES).reshape(1, LINES, 1)
    line = np.arange(LINES).reshape(1, 1, LINES)
    angle = two_pi * (((first + PARTS * second) * line) % AZ) / AZ
    real, imag = np.cos(angle) / 32.0, -np.sin(angle) / 32.0
    forward = np.concatenate(
        [np.concatenate([real, -imag], 2), np.concatenate([imag, real], 2)], 1
    )
    return forward, forward.transpose(0, 2, 1)


def fft_of(terms, sign):
    count = len(terms)
    if count == 1:
        return terms
    even, odd = fft_of(terms[::2], sign), fft_of(terms[1::2], sign)
    low, high = [], []
    for k in range(count // 2):
        re, im = odd[k]
        if k == 0:
            turned = (re, im)
        elif 4 * k == count:
            turned = (-im, re) if sign > 0 else (im, -re)
        else:
            c, s = math.cos(two_pi * k / count), sign * math.sin(two_pi * k / count)
            turned = (re * c - im * s, re * s + im * c)
        low.append((even[k][0] + turned[0], even[k][1] + turned[1]))
        high.append((even[k][0] - turned[0], even[k][1] - turned[1]))
    return low + high


def chirp_table(rate, table):
    lane = lax.broadcasted_iota(jnp.int32, (8, 2 * WIDE), 1)
    for part in range(DEPTH // WIDE):
        lag = WIDE * part - jnp.where(lane < WIDE, lane, lane - 2 * WIDE)
        inside = (lag >= 0) & (lag < PULSE)
        offset = (lag.astype(f32) - 0.5 * PULSE) / PULSE
        phase = math.pi * PULSE * rate * offset * offset
        amplitude = 1.0 / math.sqrt(PULSE)
        values = (
            jnp.where(inside, jnp.cos(phase) * amplitude, 0.0),
            jnp.where(inside, -jnp.sin(phase) * amplitude, 0.0),
        )
        for which, value in enumerate(values):
            spread = jnp.broadcast_to(value[0:1], (WIDE, 2 * WIDE))
            rolled = pltpu.roll(spread, 0, 1, stride=1, stride_axis=0)
            table[WIDE * part : WIDE * (part + 1), WIDE * which : WIDE * (which + 1)] = rolled[
                :, :WIDE
            ].astype(bf16)


def azimuth_filter(rate_row, frac, offset, filt):
    row = lax.broadcasted_iota(jnp.int32, (LINES, COLS), 0)
    half_taps = TAPS // 2
    tap_id = lax.broadcasted_iota(jnp.int32, (TAPS, COLS), 0)
    position = tap_id.astype(f32) - (half_taps - 1) - frac
    middle = position == 0.0
    turned = jnp.where(middle, 1.0, math.pi * position)
    taps = jnp.where(middle, 1.0, jnp.sin(turned) / turned)
    taps = taps * (0.5 + 0.5 * jnp.cos(math.pi * position / half_taps))
    base = row.astype(f32) * (two_pi / LINES)
    step_re, step_im = math.cos(two_pi / AZ), math.sin(two_pi / AZ)

    def one_residue(first, carry):
        zre, zim = carry
        freq = first + PARTS * row
        centered = ((freq + AZ // 2) % AZ - AZ // 2).astype(f32) / AZ
        start = ((freq * offset) % AZ).astype(f32) * (two_pi / AZ)
        phase = math.pi * AZ * rate_row * centered * centered
        re, im = jnp.cos(phase), jnp.sin(phase)
        sre, sim = jnp.cos(start), jnp.sin(start)
        re, im = re * sre - im * sim, re * sim + im * sre
        hre = jnp.broadcast_to(taps[TAPS - 1 : TAPS], (LINES, COLS))
        him = jnp.zeros((LINES, COLS), f32)
        for tap in range(TAPS - 2, -1, -1):
            hre, him = hre * zre - him * zim + taps[tap : tap + 1], hre * zim + him * zre
        filt[first, :LINES] = re * hre - im * him
        filt[first, LINES:] = re * him + im * hre
        return (zre * step_re - zim * step_im, zre * step_im + zim * step_re)

    lax.fori_loop(0, PARTS, one_residue, (jnp.cos(base), jnp.sin(base)))


def azimuth_focus(columns, filt, forward, backward, work, planes):
    step = TILE

    def spread_lines(chunk, carry):
        rows = pl.ds(pl.multiple_of(chunk * step, step), step)
        terms = [
            (columns[j, 0, rows].astype(f32), columns[j, 1, rows].astype(f32)) for j in range(PARTS)
        ]
        lower = pl.ds(pl.multiple_of(chunk * step + LINES, step), step)
        for first, (re, im) in enumerate(fft_of(terms, -1)):
            work[first, rows] = re.astype(bf16)
            work[first, lower] = im.astype(bf16)
        return carry

    lax.fori_loop(0, LINES // step, spread_lines, 0)

    def one_residue(first, carry):
        spectrum = jnp.dot(forward[first], work[first], preferred_element_type=f32)
        re, im = spectrum[:LINES], spectrum[LINES:]
        gre, gim = filt[first, :LINES], filt[first, LINES:]
        filtered = jnp.concatenate([re * gre - im * gim, re * gim + im * gre], 0).astype(bf16)
        planes[first] = jnp.dot(backward[first], filtered, preferred_element_type=f32)
        return carry

    lax.fori_loop(0, PARTS, one_residue, 0, unroll=4)


def gather_lines(wave, planes, blocks):
    rows, lower = pl.ds(TILE * wave, TILE), pl.ds(TILE * wave + LINES, TILE)
    terms = [(planes[first, rows], planes[first, lower]) for first in range(PARTS)]
    for j, (re, im) in enumerate(fft_of(terms, 1)):
        blocks[wave, j, 0] = re.astype(bf16)
        blocks[wave, j, 1] = im.astype(bf16)


MESH = pl.DeviceIdType.MESH
HALF = 16


class Place:
    def __init__(self):
        self.date, self.swath = lax.axis_index("date"), lax.axis_index("swath")
        self.side, self.spot = self.date // HALF, self.date % HALF

    def departure(self, turn):
        return (self.swath + 1 + turn) % PARTS

    def arrival(self, turn):
        return (self.swath + PARTS - turn) % PARTS


def send(source, target, leaves, lands, date, swath):
    pltpu.make_async_remote_copy(
        source, target, leaves, lands, device_id=(date, swath), device_id_type=MESH
    ).start()


def drain(block, sem):
    pltpu.make_async_copy(block, block, sem).wait()


def tell(date, swath):
    barrier = pltpu.get_barrier_semaphore()
    pl.semaphore_signal(barrier, inc=1, device_id=(date, swath), device_id_type=MESH)


def greet(place):
    def each(turn, carry):
        tell(place.date, (place.swath + turn) % PARTS)
        return carry

    lax.fori_loop(1, PARTS, each, 0)

    for ahead in (1, 2):

        @pl.when(place.spot < HALF - ahead)
        def _():
            tell(place.date + ahead, place.swath)

    for lane in range(2):

        @pl.when(place.spot != lane)
        def _():
            tell(HALF * place.side + lane, place.swath)

    @pl.when(place.spot >= HALF - 2)
    def _():
        def every(part, carry):
            tell(HALF * (1 - place.side) + (place.swath + part) % HALF, part)
            return carry

        lax.fori_loop(0, PARTS, every, 0)


def await_greetings(place):
    wanted = (
        PARTS
        + 1
        + jnp.where(place.spot != 0, 1, 0)
        + jnp.where(place.spot >= 2, 1, 0)
        + jnp.where(place.spot <= 1, HALF - 1, 0)
    )
    pl.semaphore_wait(pltpu.get_barrier_semaphore(), wanted)


def focus_kernel(
    rate_ref,
    offset_ref,
    frac_ref,
    echo_ref,
    rate_row,
    forward,
    backward,
    own,
    following,
    after,
    rims,
    table,
    extended,
    leaving,
    columns,
    filt,
    work,
    planes,
    blocks,
    crossing,
    turn_send,
    turn_recv,
    back_send,
    back_recv,
    wrap_send,
    wrap_recv,
    next_send,
    next_recv,
    last_send,
    last_recv,
    tail_send,
    rim_send,
    rim_recv,
):
    place = Place()
    greet(place)
    for which in range(SPAN + 1):
        for edge in range(2):

            @pl.when(place.swath == (PARTS - 1) * edge)
            def _():
                rims[which, edge] = jnp.zeros((PARTS, 2, TILE, COLS), bf16)

    chirp_table(rate_ref[0], table)
    for part in range(2):
        rows = slice(LINES * part, LINES * (part + 1))
        extended[rows, :RG] = echo_ref[part]
        extended[rows, RG:] = echo_ref[part, :, :PULSE]

    def one_block(block, carry):
        window = extended[:, pl.ds(pl.multiple_of(block * WIDE, WIDE), DEPTH)]
        product = jnp.dot(window, table[...], preferred_element_type=f32)
        real = product[:LINES, :WIDE] - product[LINES:, WIDE:]
        imag = product[:LINES, WIDE:] + product[LINES:, :WIDE]
        for half in range(2):
            cols = slice(COLS * half, COLS * (half + 1))
            leaving[2 * block + half, 0] = real[:, cols].astype(bf16)
            leaving[2 * block + half, 1] = imag[:, cols].astype(bf16)
        return carry

    lax.fori_loop(0, RG // WIDE, one_block, 0, unroll=2)
    await_greetings(place)

    def hand_over(turn, carry):
        goal = place.departure(turn)
        send(leaving.at[goal], columns.at[place.swath], turn_send, turn_recv, place.date, goal)
        return carry

    lax.fori_loop(0, PARTS - 1, hand_over, 0)
    kept = leaving.at[place.swath]
    pltpu.make_async_copy(kept, columns.at[place.swath], turn_recv).start()
    azimuth_filter(rate_row[...], frac_ref[0], offset_ref[0], filt)
    drain(columns, turn_recv)
    drain(leaving.at[pl.ds(0, PARTS - 1)], turn_send)

    azimuth_focus(columns, filt, forward, backward, work, planes)

    side, spot, date, swath = place.side, place.spot, place.date, place.swath
    leads = spot <= 1
    lane = spot % 2

    for wave in range(WAVES):
        gather_lines(wave, planes, blocks)

    @pl.when(leads)
    def _():
        def scatter(part, carry):
            goal = (swath + part) % HALF
            piece = blocks.at[:, part]

            @pl.when(goal != spot)
            def _():
                send(
                    piece,
                    crossing.at[lane],
                    wrap_send,
                    wrap_recv.at[lane],
                    HALF * side + goal,
                    swath,
                )

            @pl.when(goal == spot)
            def _():
                pltpu.make_async_copy(piece, crossing.at[lane], wrap_recv.at[lane]).start()

            return carry

        lax.fori_loop(0, PARTS, scatter, 0)

    def hand_back(stride):
        goal = (swath + stride) % PARTS
        send(blocks.at[:, goal], own.at[:, swath], back_send, back_recv.at[swath], date, goal)

    for stride in STRIDES[:AHEAD]:
        hand_back(stride)
    pltpu.make_async_copy(blocks.at[:, swath], own.at[:, swath], back_recv.at[swath]).start()

    has_back = spot != 0
    has_second = spot >= 2

    def pass_on(piece):
        @pl.when(has_back)
        def _():
            send(own.at[:, piece], following.at[:, piece], next_send, next_recv, date - 1, swath)

        @pl.when(has_second)
        def _():
            send(own.at[:, piece], after.at[:, piece], last_send, last_recv, date - 2, swath)

    def share_rim(which, source, wave):
        edge = 1 if wave == 0 else 0

        @pl.when(swath != (0 if wave == 0 else PARTS - 1))
        def _():
            send(
                source.at[wave],
                rims.at[which, edge],
                rim_send.at[edge],
                rim_recv.at[which, edge],
                date,
                swath - 1 if wave == 0 else swath + 1,
            )

    goal_line = (spot + HALF - swath) % HALF
    deliveries = (
        (0, following, next_recv, HALF - 1),
        (1, after, last_recv, HALF - 1),
        (0, after, last_recv, HALF - 2),
    )

    def deliver():
        for which in range(2):
            drain(crossing.at[which], wrap_recv.at[which])
        for index, (which, target, lands, goal) in enumerate(deliveries):
            send(
                crossing.at[which],
                target.at[:, swath],
                tail_send.at[index],
                lands,
                HALF * (1 - side) + goal,
                goal_line,
            )

    for turn, stride in enumerate((0,) + STRIDES):
        piece = (swath + PARTS - stride) % PARTS
        drain(own.at[:, piece], back_recv.at[piece])
        if 0 < turn and turn + AHEAD <= len(STRIDES):
            hand_back(STRIDES[turn + AHEAD - 1])
        if turn == 3:
            deliver()
        pass_on(piece)
    drain_order = ((0, own, None), (1, following, next_recv), (2, after, last_recv))
    for which, image, lands in drain_order:
        if lands is not None:
            drain(image, lands)
        for wave in ORDER[:2]:
            share_rim(which, image, wave)

    for which in range(SPAN + 1):
        for edge in range(2):

            @pl.when(swath != (PARTS - 1) * edge)
            def _():
                drain(rims.at[which, edge], rim_recv.at[which, edge])

    drain(blocks.at[:, pl.ds(0, PARTS - 1)], back_send)

    @pl.when(leads)
    def _():
        drain(blocks.at[:, pl.ds(0, HALF - 1)], wrap_send)

    @pl.when(has_back)
    def _():
        drain(own, next_send)

    @pl.when(has_second)
    def _():
        drain(own, last_send)

    for index, (which, target, lands, goal) in enumerate(deliveries):
        drain(crossing.at[which], tail_send.at[index])

    for edge in range(2):

        @pl.when(swath != (PARTS - 1) * (1 - edge))
        def _():
            drain(own.at[pl.ds(0, SPAN + 1)], rim_send.at[edge])


def line_sums():
    line = np.arange(LINES)[:, None]
    row = np.arange(ROWS)[None, :]
    place = np.where(row < LINES, row, np.where(row < LINES + 8, row - LINES - 8, row - 8))
    return (np.abs(place - line) <= WIN_AZ // 2).astype(np.float32)


def sample_sums():
    sample = np.arange(2 * WIDE)[:, None]
    middle = np.arange(WIDE)[None, :] + PAD
    return (np.abs(sample - middle) <= WIN_RG // 2).astype(np.float32)


def coherence_kernel(
    lines_ref,
    samples_ref,
    own_ref,
    next_ref,
    after_ref,
    rims_ref,
    image_ref,
    result_ref,
    held,
):
    edge = jnp.zeros((7 * LINES, PAD), bf16)
    held[:, :PAD] = edge
    held[:, PAD + RG :] = edge
    sums = lines_ref[...]

    def one_piece(piece, carry):
        def lines_of(which, image, part):
            tiles = [image[wave, piece, part].astype(f32) for wave in range(WAVES)]
            tiles.append(rims_ref[which, 0, piece, part].astype(f32)[8:])
            tiles.append(rims_ref[which, 1, piece, part].astype(f32)[:8])
            return jnp.concatenate(tiles, 0)

        are, aim = lines_of(0, own_ref, 0), lines_of(0, own_ref, 1)
        maps = [are * are + aim * aim]
        for which, other in ((1, next_ref), (2, after_ref)):
            bre, bim = lines_of(which, other, 0), lines_of(which, other, 1)
            maps += [bre * bre + bim * bim, are * bre + aim * bim, aim * bre - are * bim]
        lanes = pl.ds(pl.multiple_of(piece * COLS, COLS), COLS)
        stacked = jnp.concatenate([m.astype(bf16) for m in maps], 1)
        summed = jnp.dot(sums, stacked, preferred_element_type=f32)
        inner = pl.ds(pl.multiple_of(piece * COLS + PAD, COLS), COLS)
        for which in range(7):
            held[LINES * which : LINES * (which + 1), inner] = summed[
                :, COLS * which : COLS * (which + 1)
            ].astype(bf16)
        for part in range(2):
            for wave in range(WAVES):
                rows = slice(TILE * wave, TILE * (wave + 1))
                image_ref[0, part, rows, lanes] = own_ref[wave, piece, part]
        return carry

    lax.fori_loop(0, PARTS, one_piece, 0, unroll=4)

    def one_span(span, carry):
        start = pl.multiple_of(span * WIDE, WIDE)
        window = held[:, pl.ds(start, 2 * WIDE)]
        boxes = jnp.dot(window, samples_ref[...], preferred_element_type=f32)
        box = [boxes[LINES * which : LINES * (which + 1)] for which in range(7)]
        for pair in range(SPAN):
            scale = lax.rsqrt(box[0] * box[3 * pair + 1] + epsilon)
            for part in range(2):
                term = box[3 * pair + 2 + part] * scale
                result_ref[0, pair, part, :, pl.ds(start, WIDE)] = term.astype(bf16)
        return carry

    lax.fori_loop(0, RG // WIDE, one_span, 0, unroll=2)


def vmem(count):
    return [pl.BlockSpec(memory_space=pltpu.VMEM)] * count


def params(**more):
    return pltpu.CompilerParams(vmem_limit_bytes=56 * 1024 * 1024, **more)


def coherence_call(own, following, after, rims):
    return pl.pallas_call(
        coherence_kernel,
        out_shape=(
            jax.ShapeDtypeStruct((1, 2, LINES, RG), bf16),
            jax.ShapeDtypeStruct((1, SPAN, 2, LINES, RG), bf16),
        ),
        in_specs=vmem(6),
        out_specs=tuple(vmem(2)),
        scratch_shapes=[pltpu.VMEM((7 * LINES, RG + 2 * PAD), bf16)],
        compiler_params=params(),
    )(
        jnp.asarray(line_sums(), bf16),
        jnp.asarray(sample_sums(), bf16),
        own,
        following,
        after,
        rims,
    )


def focus_call(raw_echo, range_rate, azimuth_rate, line_offset, frac_shift):
    forward, backward = mini_dft()
    dma = pltpu.SemaphoreType.DMA
    return pl.pallas_call(
        focus_kernel,
        out_shape=(jax.ShapeDtypeStruct((WAVES, PARTS, 2, TILE, COLS), bf16),) * 3
        + (jax.ShapeDtypeStruct((SPAN + 1, 2, PARTS, 2, TILE, COLS), bf16),),
        in_specs=[pl.BlockSpec(memory_space=pltpu.SMEM)] * 3 + vmem(4),
        out_specs=tuple(vmem(4)),
        scratch_shapes=[
            pltpu.VMEM((DEPTH, 2 * WIDE), bf16),
            pltpu.VMEM((2 * LINES, RG + PULSE), bf16),
            pltpu.VMEM((PARTS, 2, LINES, COLS), bf16),
            pltpu.VMEM((PARTS, 2, LINES, COLS), bf16),
            pltpu.VMEM((PARTS, 2 * LINES, COLS), f32),
            pltpu.VMEM((PARTS, 2 * LINES, COLS), bf16),
            pltpu.VMEM((PARTS, 2 * LINES, COLS), f32),
            pltpu.VMEM((WAVES, PARTS, 2, TILE, COLS), bf16),
            pltpu.VMEM((2, WAVES, 2, TILE, COLS), bf16),
            dma,
            dma,
            dma,
            dma((PARTS,)),
            dma,
            dma((2,)),
            dma,
            dma,
            dma,
            dma,
            dma((3,)),
            dma((2,)),
            dma((SPAN + 1, 2)),
        ],
        compiler_params=params(collective_id=0, has_side_effects=True),
    )(
        range_rate.reshape(1),
        line_offset,
        frac_shift,
        raw_echo[0],
        azimuth_rate.reshape(1, COLS),
        jnp.asarray(forward, bf16),
        jnp.asarray(backward, bf16),
    )


def body(raw_echo, range_rate, azimuth_rate, line_offset, frac_shift):
    return coherence_call(
        *focus_call(raw_echo, range_rate, azimuth_rate, line_offset, frac_shift)
    )


def solution(mesh):
    placed = (P("date", None, "swath", None), P(), P("swath"), P("date"), P("date"))
    return jax.shard_map(
        body,
        mesh=mesh,
        in_specs=placed,
        out_specs=(P("date", None, "swath", None), P("date", None, None, "swath", None)),
        check_vma=False,
    )
```

```python
import functools
import math

import numpy as np
import jax
import jax.numpy as jnp
from jax import lax
from jax.experimental import pallas as pl
from jax.experimental.pallas import tpu as pltpu
from jax.sharding import PartitionSpec as P

AZ = 1024
RG = 2048
TAPS = 8
WIN_AZ = 11
WIN_RG = 5
SPAN = 2
PARTS = 16
LINES = AZ // PARTS
COLS = RG // PARTS
ROWS = LINES + 16
TILE = 16
WAVES = LINES // TILE
ORDER = (0, WAVES - 1) + tuple(range(1, WAVES - 1))
STRIDES = (8, 7, 4, 1, 15, 9, 10, 5, 2, 14, 6, 11, 12, 3, 13)
AHEAD = 5
PULSE = RG // 2
WIDE = 256
DEPTH = PULSE + WIDE
PAD = 128

two_pi = 2.0 * math.pi
epsilon = 1e-06
f32 = jnp.float32
bf16 = jnp.bfloat16


def mini_dft():
    first = np.arange(PARTS).reshape(PARTS, 1, 1)
    second = np.arange(LINES).reshape(1, LINES, 1)
    line = np.arange(LINES).reshape(1, 1, LINES)
    angle = two_pi * (((first + PARTS * second) * line) % AZ) / AZ
    real, imag = np.cos(angle) / 32.0, -np.sin(angle) / 32.0
    forward = np.concatenate(
        [np.concatenate([real, -imag], 2), np.concatenate([imag, real], 2)], 1
    )
    return forward, forward.transpose(0, 2, 1)


def fft_of(terms, sign):
    count = len(terms)
    if count == 1:
        return terms
    even, odd = fft_of(terms[::2], sign), fft_of(terms[1::2], sign)
    low, high = [], []
    for k in range(count // 2):
        re, im = odd[k]
        if k == 0:
            turned = (re, im)
        elif 4 * k == count:
            turned = (-im, re) if sign > 0 else (im, -re)
        else:
            c, s = math.cos(two_pi * k / count), sign * math.sin(two_pi * k / count)
            turned = (re * c - im * s, re * s + im * c)
        low.append((even[k][0] + turned[0], even[k][1] + turned[1]))
        high.append((even[k][0] - turned[0], even[k][1] - turned[1]))
    return low + high


def chirp_table(rate, table):
    lane = lax.broadcasted_iota(jnp.int32, (8, 2 * WIDE), 1)
    for part in range(DEPTH // WIDE):
        lag = WIDE * part - jnp.where(lane < WIDE, lane, lane - 2 * WIDE)
        inside = (lag >= 0) & (lag < PULSE)
        offset = (lag.astype(f32) - 0.5 * PULSE) / PULSE
        phase = math.pi * PULSE * rate * offset * offset
        amplitude = 1.0 / math.sqrt(PULSE)
        values = (
            jnp.where(inside, jnp.cos(phase) * amplitude, 0.0),
            jnp.where(inside, -jnp.sin(phase) * amplitude, 0.0),
        )
        for which, value in enumerate(values):
            spread = jnp.broadcast_to(value[0:1], (WIDE, 2 * WIDE))
            rolled = pltpu.roll(spread, 0, 1, stride=1, stride_axis=0)
            table[WIDE * part : WIDE * (part + 1), WIDE * which : WIDE * (which + 1)] = rolled[
                :, :WIDE
            ].astype(bf16)


def azimuth_filter(rate_row, frac, offset, filt):
    row = lax.broadcasted_iota(jnp.int32, (LINES, COLS), 0)
    half_taps = TAPS // 2
    tap_id = lax.broadcasted_iota(jnp.int32, (TAPS, COLS), 0)
    position = tap_id.astype(f32) - (half_taps - 1) - frac
    middle = position == 0.0
    turned = jnp.where(middle, 1.0, math.pi * position)
    taps = jnp.where(middle, 1.0, jnp.sin(turned) / turned)
    taps = taps * (0.5 + 0.5 * jnp.cos(math.pi * position / half_taps))
    base = row.astype(f32) * (two_pi / LINES)
    step_re, step_im = math.cos(two_pi / AZ), math.sin(two_pi / AZ)

    def one_residue(first, carry):
        zre, zim = carry
        freq = first + PARTS * row
        centered = ((freq + AZ // 2) % AZ - AZ // 2).astype(f32) / AZ
        start = ((freq * offset) % AZ).astype(f32) * (two_pi / AZ)
        phase = math.pi * AZ * rate_row * centered * centered
        re, im = jnp.cos(phase), jnp.sin(phase)
        sre, sim = jnp.cos(start), jnp.sin(start)
        re, im = re * sre - im * sim, re * sim + im * sre
        hre = jnp.broadcast_to(taps[TAPS - 1 : TAPS], (LINES, COLS))
        him = jnp.zeros((LINES, COLS), f32)
        for tap in range(TAPS - 2, -1, -1):
            hre, him = hre * zre - him * zim + taps[tap : tap + 1], hre * zim + him * zre
        filt[first, :LINES] = re * hre - im * him
        filt[first, LINES:] = re * him + im * hre
        return (zre * step_re - zim * step_im, zre * step_im + zim * step_re)

    lax.fori_loop(0, PARTS, one_residue, (jnp.cos(base), jnp.sin(base)))


def azimuth_focus(columns, filt, forward, backward, work, planes):
    step = TILE

    def spread_lines(chunk, carry):
        rows = pl.ds(pl.multiple_of(chunk * step, step), step)
        terms = [
            (columns[j, 0, rows].astype(f32), columns[j, 1, rows].astype(f32)) for j in range(PARTS)
        ]
        lower = pl.ds(pl.multiple_of(chunk * step + LINES, step), step)
        for first, (re, im) in enumerate(fft_of(terms, -1)):
            work[first, rows] = re.astype(bf16)
            work[first, lower] = im.astype(bf16)
        return carry

    lax.fori_loop(0, LINES // step, spread_lines, 0)

    def one_residue(first, carry):
        spectrum = jnp.dot(forward[first], work[first], preferred_element_type=f32)
        re, im = spectrum[:LINES], spectrum[LINES:]
        gre, gim = filt[first, :LINES], filt[first, LINES:]
        filtered = jnp.concatenate([re * gre - im * gim, re * gim + im * gre], 0).astype(bf16)
        planes[first] = jnp.dot(backward[first], filtered, preferred_element_type=f32)
        return carry

    lax.fori_loop(0, PARTS, one_residue, 0, unroll=8)


def gather_lines(wave, planes, blocks):
    rows, lower = pl.ds(TILE * wave, TILE), pl.ds(TILE * wave + LINES, TILE)
    terms = [(planes[first, rows], planes[first, lower]) for first in range(PARTS)]
    for j, (re, im) in enumerate(fft_of(terms, 1)):
        blocks[wave, j, 0] = re.astype(bf16)
        blocks[wave, j, 1] = im.astype(bf16)


MESH = pl.DeviceIdType.MESH
HALF = 16


class Place:
    def __init__(self):
        self.date, self.swath = lax.axis_index("date"), lax.axis_index("swath")
        self.side, self.spot = self.date // HALF, self.date % HALF

    def departure(self, turn):
        return (self.swath + 1 + turn) % PARTS

    def arrival(self, turn):
        return (self.swath + PARTS - turn) % PARTS


def send(source, target, leaves, lands, date, swath):
    pltpu.make_async_remote_copy(
        source, target, leaves, lands, device_id=(date, swath), device_id_type=MESH
    ).start()


def drain(block, sem):
    pltpu.make_async_copy(block, block, sem).wait()


def tell(date, swath):
    barrier = pltpu.get_barrier_semaphore()
    pl.semaphore_signal(barrier, inc=1, device_id=(date, swath), device_id_type=MESH)


def greet(place):
    def each(turn, carry):
        tell(place.date, (place.swath + turn) % PARTS)
        return carry

    lax.fori_loop(1, PARTS, each, 0)

    for ahead in (1, 2):

        @pl.when(place.spot < HALF - ahead)
        def _():
            tell(place.date + ahead, place.swath)

    for lane in range(2):

        @pl.when(place.spot != lane)
        def _():
            tell(HALF * place.side + lane, place.swath)

    @pl.when(place.spot >= HALF - 2)
    def _():
        def every(part, carry):
            tell(HALF * (1 - place.side) + (place.swath + part) % HALF, part)
            return carry

        lax.fori_loop(0, PARTS, every, 0)


def await_greetings(place):
    wanted = (
        PARTS
        + 1
        + jnp.where(place.spot != 0, 1, 0)
        + jnp.where(place.spot >= 2, 1, 0)
        + jnp.where(place.spot <= 1, HALF - 1, 0)
    )
    pl.semaphore_wait(pltpu.get_barrier_semaphore(), wanted)


def focus_kernel(
    rate_ref,
    offset_ref,
    frac_ref,
    echo_ref,
    rate_row,
    forward,
    backward,
    own,
    following,
    after,
    rims,
    table,
    extended,
    leaving,
    columns,
    filt,
    work,
    planes,
    blocks,
    crossing,
    turn_send,
    turn_recv,
    back_send,
    back_recv,
    wrap_send,
    wrap_recv,
    next_send,
    next_recv,
    last_send,
    last_recv,
    tail_send,
    rim_send,
    rim_recv,
):
    place = Place()
    greet(place)
    for which in range(SPAN + 1):
        for edge in range(2):

            @pl.when(place.swath == (PARTS - 1) * edge)
            def _():
                rims[which, edge] = jnp.zeros((PARTS, 2, TILE, COLS), bf16)

    chirp_table(rate_ref[0], table)
    for part in range(2):
        rows = slice(LINES * part, LINES * (part + 1))
        extended[rows, :RG] = echo_ref[part]
        extended[rows, RG:] = echo_ref[part, :, :PULSE]

    def one_block(block, carry):
        window = extended[:, pl.ds(pl.multiple_of(block * WIDE, WIDE), DEPTH)]
        product = jnp.dot(window, table[...], preferred_element_type=f32)
        real = product[:LINES, :WIDE] - product[LINES:, WIDE:]
        imag = product[:LINES, WIDE:] + product[LINES:, :WIDE]
        for half in range(2):
            cols = slice(COLS * half, COLS * (half + 1))
            leaving[2 * block + half, 0] = real[:, cols].astype(bf16)
            leaving[2 * block + half, 1] = imag[:, cols].astype(bf16)
        return carry

    lax.fori_loop(0, RG // WIDE, one_block, 0, unroll=4)
    await_greetings(place)

    def hand_over(turn, carry):
        goal = place.departure(turn)
        send(leaving.at[goal], columns.at[place.swath], turn_send, turn_recv, place.date, goal)
        return carry

    lax.fori_loop(0, PARTS - 1, hand_over, 0)
    kept = leaving.at[place.swath]
    pltpu.make_async_copy(kept, columns.at[place.swath], turn_recv).start()
    azimuth_filter(rate_row[...], frac_ref[0], offset_ref[0], filt)
    drain(columns, turn_recv)
    drain(leaving.at[pl.ds(0, PARTS - 1)], turn_send)

    azimuth_focus(columns, filt, forward, backward, work, planes)

    side, spot, date, swath = place.side, place.spot, place.date, place.swath
    leads = spot <= 1
    lane = spot % 2

    for wave in range(WAVES):
        gather_lines(wave, planes, blocks)

    @pl.when(leads)
    def _():
        def scatter(part, carry):
            goal = (swath + part) % HALF
            piece = blocks.at[:, part]

            @pl.when(goal != spot)
            def _():
                send(
                    piece,
                    crossing.at[lane],
                    wrap_send,
                    wrap_recv.at[lane],
                    HALF * side + goal,
                    swath,
                )

            @pl.when(goal == spot)
            def _():
                pltpu.make_async_copy(piece, crossing.at[lane], wrap_recv.at[lane]).start()

            return carry

        lax.fori_loop(0, PARTS, scatter, 0)

    def hand_back(stride):
        goal = (swath + stride) % PARTS
        send(blocks.at[:, goal], own.at[:, swath], back_send, back_recv.at[swath], date, goal)

    for stride in STRIDES[:AHEAD]:
        hand_back(stride)
    pltpu.make_async_copy(blocks.at[:, swath], own.at[:, swath], back_recv.at[swath]).start()

    has_back = spot != 0
    has_second = spot >= 2

    def pass_on(piece):
        @pl.when(has_back)
        def _():
            send(own.at[:, piece], following.at[:, piece], next_send, next_recv, date - 1, swath)

        @pl.when(has_second)
        def _():
            send(own.at[:, piece], after.at[:, piece], last_send, last_recv, date - 2, swath)

    def share_rim(which, source, wave):
        edge = 1 if wave == 0 else 0

        @pl.when(swath != (0 if wave == 0 else PARTS - 1))
        def _():
            send(
                source.at[wave],
                rims.at[which, edge],
                rim_send.at[edge],
                rim_recv.at[which, edge],
                date,
                swath - 1 if wave == 0 else swath + 1,
            )

    goal_line = (spot + HALF - swath) % HALF
    deliveries = (
        (0, following, next_recv, HALF - 1),
        (1, after, last_recv, HALF - 1),
        (0, after, last_recv, HALF - 2),
    )

    def deliver():
        for which in range(2):
            drain(crossing.at[which], wrap_recv.at[which])
        for index, (which, target, lands, goal) in enumerate(deliveries):
            send(
                crossing.at[which],
                target.at[:, swath],
                tail_send.at[index],
                lands,
                HALF * (1 - side) + goal,
                goal_line,
            )

    for turn, stride in enumerate((0,) + STRIDES):
        piece = (swath + PARTS - stride) % PARTS
        drain(own.at[:, piece], back_recv.at[piece])
        if 0 < turn and turn + AHEAD <= len(STRIDES):
            hand_back(STRIDES[turn + AHEAD - 1])
        if turn == 3:
            deliver()
        pass_on(piece)
    drain_order = ((0, own, None), (1, following, next_recv), (2, after, last_recv))
    for which, image, lands in drain_order:
        if lands is not None:
            drain(image, lands)
        for wave in ORDER[:2]:
            share_rim(which, image, wave)

    for which in range(SPAN + 1):
        for edge in range(2):

            @pl.when(swath != (PARTS - 1) * edge)
            def _():
                drain(rims.at[which, edge], rim_recv.at[which, edge])

    drain(blocks.at[:, pl.ds(0, PARTS - 1)], back_send)

    @pl.when(leads)
    def _():
        drain(blocks.at[:, pl.ds(0, HALF - 1)], wrap_send)

    @pl.when(has_back)
    def _():
        drain(own, next_send)

    @pl.when(has_second)
    def _():
        drain(own, last_send)

    for index, (which, target, lands, goal) in enumerate(deliveries):
        drain(crossing.at[which], tail_send.at[index])

    for edge in range(2):

        @pl.when(swath != (PARTS - 1) * (1 - edge))
        def _():
            drain(own.at[pl.ds(0, SPAN + 1)], rim_send.at[edge])


def line_sums():
    line = np.arange(LINES)[:, None]
    row = np.arange(ROWS)[None, :]
    place = np.where(row < LINES, row, np.where(row < LINES + 8, row - LINES - 8, row - 8))
    return (np.abs(place - line) <= WIN_AZ // 2).astype(np.float32)


def sample_sums():
    sample = np.arange(2 * WIDE)[:, None]
    middle = np.arange(WIDE)[None, :] + PAD
    return (np.abs(sample - middle) <= WIN_RG // 2).astype(np.float32)


def coherence_kernel(
    lines_ref,
    samples_ref,
    own_ref,
    next_ref,
    after_ref,
    rims_ref,
    image_ref,
    result_ref,
    held,
):
    edge = jnp.zeros((7 * LINES, PAD), bf16)
    held[:, :PAD] = edge
    held[:, PAD + RG :] = edge
    sums = lines_ref[...]

    def one_piece(piece, carry):
        def lines_of(which, image, part):
            tiles = [image[wave, piece, part].astype(f32) for wave in range(WAVES)]
            tiles.append(rims_ref[which, 0, piece, part].astype(f32)[8:])
            tiles.append(rims_ref[which, 1, piece, part].astype(f32)[:8])
            return jnp.concatenate(tiles, 0)

        are, aim = lines_of(0, own_ref, 0), lines_of(0, own_ref, 1)
        maps = [are * are + aim * aim]
        for which, other in ((1, next_ref), (2, after_ref)):
            bre, bim = lines_of(which, other, 0), lines_of(which, other, 1)
            maps += [bre * bre + bim * bim, are * bre + aim * bim, aim * bre - are * bim]
        lanes = pl.ds(pl.multiple_of(piece * COLS, COLS), COLS)
        stacked = jnp.concatenate([m.astype(bf16) for m in maps], 1)
        summed = jnp.dot(sums, stacked, preferred_element_type=f32)
        inner = pl.ds(pl.multiple_of(piece * COLS + PAD, COLS), COLS)
        for which in range(7):
            held[LINES * which : LINES * (which + 1), inner] = summed[
                :, COLS * which : COLS * (which + 1)
            ].astype(bf16)
        for part in range(2):
            for wave in range(WAVES):
                rows = slice(TILE * wave, TILE * (wave + 1))
                image_ref[0, part, rows, lanes] = own_ref[wave, piece, part]
        return carry

    lax.fori_loop(0, PARTS, one_piece, 0, unroll=8)

    def one_span(span, carry):
        start = pl.multiple_of(span * WIDE, WIDE)
        window = held[:, pl.ds(start, 2 * WIDE)]
        boxes = jnp.dot(window, samples_ref[...], preferred_element_type=f32)
        box = [boxes[LINES * which : LINES * (which + 1)] for which in range(7)]
        for pair in range(SPAN):
            scale = lax.rsqrt(box[0] * box[3 * pair + 1] + epsilon)
            for part in range(2):
                term = box[3 * pair + 2 + part] * scale
                result_ref[0, pair, part, :, pl.ds(start, WIDE)] = term.astype(bf16)
        return carry

    lax.fori_loop(0, RG // WIDE, one_span, 0, unroll=4)


def vmem(count):
    return [pl.BlockSpec(memory_space=pltpu.VMEM)] * count


def params(**more):
    return pltpu.CompilerParams(vmem_limit_bytes=56 * 1024 * 1024, **more)


def coherence_call(own, following, after, rims):
    return pl.pallas_call(
        coherence_kernel,
        out_shape=(
            jax.ShapeDtypeStruct((1, 2, LINES, RG), bf16),
            jax.ShapeDtypeStruct((1, SPAN, 2, LINES, RG), bf16),
        ),
        in_specs=vmem(6),
        out_specs=tuple(vmem(2)),
        scratch_shapes=[pltpu.VMEM((7 * LINES, RG + 2 * PAD), bf16)],
        compiler_params=params(),
    )(
        jnp.asarray(line_sums(), bf16),
        jnp.asarray(sample_sums(), bf16),
        own,
        following,
        after,
        rims,
    )


def focus_call(raw_echo, range_rate, azimuth_rate, line_offset, frac_shift):
    forward, backward = mini_dft()
    dma = pltpu.SemaphoreType.DMA
    return pl.pallas_call(
        focus_kernel,
        out_shape=(jax.ShapeDtypeStruct((WAVES, PARTS, 2, TILE, COLS), bf16),) * 3
        + (jax.ShapeDtypeStruct((SPAN + 1, 2, PARTS, 2, TILE, COLS), bf16),),
        in_specs=[pl.BlockSpec(memory_space=pltpu.SMEM)] * 3 + vmem(4),
        out_specs=tuple(vmem(4)),
        scratch_shapes=[
            pltpu.VMEM((DEPTH, 2 * WIDE), bf16),
            pltpu.VMEM((2 * LINES, RG + PULSE), bf16),
            pltpu.VMEM((PARTS, 2, LINES, COLS), bf16),
            pltpu.VMEM((PARTS, 2, LINES, COLS), bf16),
            pltpu.VMEM((PARTS, 2 * LINES, COLS), f32),
            pltpu.VMEM((PARTS, 2 * LINES, COLS), bf16),
            pltpu.VMEM((PARTS, 2 * LINES, COLS), f32),
            pltpu.VMEM((WAVES, PARTS, 2, TILE, COLS), bf16),
            pltpu.VMEM((2, WAVES, 2, TILE, COLS), bf16),
            dma,
            dma,
            dma,
            dma((PARTS,)),
            dma,
            dma((2,)),
            dma,
            dma,
            dma,
            dma,
            dma((3,)),
            dma((2,)),
            dma((SPAN + 1, 2)),
        ],
        compiler_params=params(collective_id=0, has_side_effects=True),
    )(
        range_rate.reshape(1),
        line_offset,
        frac_shift,
        raw_echo[0],
        azimuth_rate.reshape(1, COLS),
        jnp.asarray(forward, bf16),
        jnp.asarray(backward, bf16),
    )


def body(raw_echo, range_rate, azimuth_rate, line_offset, frac_shift):
    return coherence_call(
        *focus_call(raw_echo, range_rate, azimuth_rate, line_offset, frac_shift)
    )


def solution(mesh):
    placed = (P("date", None, "swath", None), P(), P("swath"), P("date"), P("date"))
    return jax.shard_map(
        body,
        mesh=mesh,
        in_specs=placed,
        out_specs=(P("date", None, "swath", None), P("date", None, None, "swath", None)),
        check_vma=False,
    )
```
